32 devices in a mesh: run: 4 (over z), cell: 8 (over y, x, core).
Axes of the slice: x: 2, y: 2, z: 4, core: 2. Of those that a mesh axis runs over, the one named last changes fastest.
Arguments:
- outputs: bfloat16 [4096, 4, 4096], P('run', None, 'cell'), may hold values from -6 to 6
- run_precision: bfloat16 [4096, 4096], P('run', 'cell'), as said below
- line_precision: bfloat16 [4096, 4096], P(None, 'cell'), as said below
Outputs:
- weights: bfloat16 [4096, 4, 4096], P('run', None, 'cell')
The draws below stay inside these ranges and needn't reach their ends.
Inputs may be any that keep to these rules, and one draw needn't show every extreme that they name: run_precision is symmetric. line_precision is symmetric.
All inputs are finite; a program needn't handle non-finite values.
Results may differ from the reference program's by a relative error of at most 0.0049.
Values may be sent and summed in bfloat16 or wider, within the bound.
A program may use at most 128 MiB of HBM per device.

```python
import math
import jax
import jax.numpy as jnp

RUNS = 4096
NY = 4096
LINES = 4


def precision_matrix(key, order):
    first, second = jax.random.split(key, 2)
    noise = jax.random.normal(first, (order, order), jnp.float32) * math.sqrt(0.5 / order)
    symmetric = (noise + noise.T) * math.sqrt(0.5)
    diagonal = jax.random.uniform(second, (order,), jnp.float32, 0.5, 1.5)
    matrix = symmetric + jnp.diag(diagonal)
    return matrix.astype(jnp.bfloat16)


def draw_run_precision(key, part):
    return precision_matrix(jax.random.fold_in(key, 11), RUNS)


def draw_line_precision(key, part):
    return precision_matrix(jax.random.fold_in(key, 23), NY)


def block_levels(key, dims, cuts, low, high):
    loudness, own = 1.0, jax.random.fold_in(key, 6)
    for axis_at, shards_of in cuts:
        draws = jnp.exp(jax.random.uniform(jax.random.fold_in(own, axis_at), (shards_of,), jnp.float32, low / len(cuts), high / len(cuts)))
        loudness = loudness * jnp.repeat(draws, dims[axis_at] // shards_of).reshape([-1 if axis == axis_at else 1 for axis in range(len(dims))])
    return loudness


def gaussian(stream_key, shape, width, bound, cuts=(), dtype=jnp.bfloat16):
    factor_of = block_levels(stream_key, shape, cuts, -0.22, 0.18) if cuts else 1.0
    result = jax.random.normal(stream_key, shape, jnp.float32) * width * factor_of
    return jnp.minimum(jnp.maximum(result, -bound), bound).astype(dtype)


def setup_inputs(seed: int = 0) -> dict:
    seeds = jax.random.split(jax.random.key(seed), 4)
    return {
        "outputs": gaussian(seeds[0], (RUNS, LINES, NY), 1.0, 6.0, ((0, 4), (2, 8))),
        "run_precision": draw_run_precision(jax.random.fold_in(seeds[3], 71), 0),
        "line_precision": draw_line_precision(jax.random.fold_in(seeds[3], 71), 0),
    }


def reference(outputs, run_precision, line_precision):
    flat_cells = outputs.reshape(RUNS, LINES * NY)
    middle = jnp.dot(run_precision, flat_cells, preferred_element_type=jnp.float32).astype(jnp.bfloat16)
    weighted = jnp.dot(middle.reshape(RUNS * LINES, NY), line_precision, preferred_element_type=jnp.float32)
    return weighted.astype(jnp.bfloat16).reshape(RUNS, LINES, NY)
```

```python
import jax
import jax.numpy as jnp
from jax import lax
from jax.sharding import PartitionSpec as P


def dot(a, b, contract=(1, 0)):
    return lax.dot_general(
        a, b, (((contract[0],), (contract[1],)), ((), ())), preferred_element_type=jnp.float32
    )


def bit_orders(cells):
    bits = []
    bit = cells // 2
    while bit > 1:
        bits.append(bit)
        bit //= 2
    half = len(bits) // 2
    return bits, bits[half:] + bits[:half]


def held_masks(cells):
    own = []
    for order in bit_orders(cells):
        masks = [0]
        for bit in order:
            masks = masks + [m ^ bit for m in masks]
        own.append(masks)
    return [own[0] + [m ^ 1 for m in own[1]], own[1] + [m ^ 1 for m in own[0]]]


def make_per_device(runs, cells):
    order0, order1 = bit_orders(cells)
    masks = held_masks(cells)
    half = runs // 2

    def flip_run(value, mask):
        return lax.ppermute(value, "run", [(i, i ^ mask) for i in range(runs)])

    def flip_core(value):
        return lax.ppermute(value, "cell", [(c, c ^ 1) for c in range(cells)])

    def gather_cells(block):
        pieces = [block]
        for bit0, bit1 in zip(order0, order1):
            pairs = [(c, c ^ (bit1 if c % 2 else bit0)) for c in range(cells)]
            pieces = pieces + [lax.ppermute(p, "cell", pairs) for p in pieces]
        mine = jnp.concatenate(pieces, axis=1)
        return mine, flip_core(mine)

    def per_device(outputs, run_precision, line_precision):
        rows, line_count, width = outputs.shape
        run = lax.axis_index("run")
        cell = lax.axis_index("cell")
        core = lax.rem(cell, 2)
        table = jnp.asarray(masks, jnp.int32)[core]
        held = jnp.bitwise_xor(table, cell)
        place = jnp.argsort(held)

        lines = [outputs[:, i, :] for i in range(line_count)]
        early = line_count // 2

        blocks = [
            lax.dynamic_slice_in_dim(line_precision, held[t] * width, width, axis=0)
            for t in range(cells)
        ]
        b_mine = jnp.concatenate(blocks[: cells // 2], axis=0)
        b_other = jnp.concatenate(blocks[cells // 2 :], axis=0)

        def along_line(block):
            mine, other = gather_cells(block)
            return (dot(mine, b_mine) + dot(other, b_other)).astype(block.dtype)

        far = [flip_run(lines[i], half) for i in range(early)]

        mine, other = gather_cells(run_precision)
        pieces = [
            lax.slice_in_dim(part, t * width, (t + 1) * width, axis=1)
            for part in (mine, other)
            for t in range(cells // 2)
        ]
        stacked = jnp.stack(pieces)
        own_rows = jnp.concatenate(
            [lax.dynamic_index_in_dim(stacked, place[j], 0, keepdims=False) for j in range(cells)],
            axis=1,
        )

        def columns(of_run, start=0, size=rows):
            return lax.dynamic_slice_in_dim(own_rows, of_run * rows + start, size, axis=1)

        a_near = columns(run)
        a_far = columns(run ^ half)
        near_t, far_of = [], []
        for k in range(1, half):
            near_t.append(columns(run ^ k))
            sent = columns(run ^ k ^ half, core * (rows // 2), rows // 2)
            got = flip_run(sent, k)
            got2 = flip_core(got)
            far_of.append(
                jnp.where(
                    core == 0,
                    jnp.concatenate([got, got2], axis=1),
                    jnp.concatenate([got2, got], axis=1),
                )
            )

        def along_runs(near, far_block):
            got = []
            for k in range(1, half):
                part = dot(near_t[k - 1], near, (0, 0)) + dot(far_of[k - 1], far_block)
                got.append(flip_run(part.astype(near.dtype), k))
            total = dot(a_near, near) + dot(a_far, far_block)
            for g in got:
                total = total + g.astype(jnp.float32)
            return total.astype(near.dtype)

        late = [along_line(lines[i]) for i in range(early, line_count)]
        middle = [along_runs(lines[i], far[i]) for i in range(early)]
        first = [along_line(m) for m in middle]
        last = [along_runs(w, flip_run(w, half)) for w in late]
        return jnp.stack(first + last, axis=1)

    return per_device


def solution(mesh):
    placed = (P("run", None, "cell"), P("run", "cell"), P(None, "cell"))
    return jax.shard_map(
        make_per_device(mesh.shape["run"], mesh.shape["cell"]),
        mesh=mesh,
        in_specs=placed,
        out_specs=P("run", None, "cell"),
        check_vma=False,
    )
```
